32 devices in a mesh: param: 8 (over y, x, core), ex: 4 (over z).
Axes of the slice: x: 2, y: 2, z: 4, core: 2. Of those that a mesh axis runs over, the one named last changes fastest.
Arguments:
- grads: float32 [49152, 2048], P('param', 'ex'), may hold values from -6 to 6
- projection: bfloat16 [49152, 1024], P('param'), may hold values from -6 to 6
- whitener: float32 [1024, 1024], P('param'), may hold values from -1 to 3
Outputs:
- scores: float32 [2048, 2048], P('ex', 'param')
The draws below stay inside these ranges and needn't reach their ends.
All inputs are finite; a program needn't handle non-finite values.
Results may differ from the reference program's by a relative error of at most 0.0052.
Values may be sent and summed in bfloat16 or wider, within the bound.
A program may use at most 128 MiB of HBM per device.

```python
import math
import jax
import jax.numpy as jnp
from jax import lax

K = 1024
PARAMS = 49152
EXAMPLES = 2048


def draw_whitener(key, part):
    first_key = jax.random.fold_in(key, 11)
    second_key = jax.random.fold_in(key, 23)
    diagonal = jnp.exp(jax.random.uniform(first_key, (K,), jnp.float32, -0.7, 0.7))
    off_part = jax.random.normal(second_key, (K, K), jnp.float32) * (0.5 / jnp.sqrt(1.0 * K))
    off_part = jnp.clip(off_part, -0.9, 0.9)
    return off_part + jnp.diag(diagonal)


def level_of(rng, extent, split, least, largest):
    def one(dim, blocks):
        steps = jax.random.uniform(jax.random.fold_in(jax.random.fold_in(rng, 6), dim), (blocks,), jnp.float32, least / len(split), largest / len(split))
        return jnp.repeat(jnp.exp(steps), extent[dim] // blocks).reshape((-1,) + (1,) * (len(extent) - dim - 1))

    gain = one(*split[0])
    for cut in split[1:]:
        gain = gain * one(*cut)
    return gain


def noise(stream_key, dims, scale, most, split=(), dtype=jnp.bfloat16):
    drawn = scale * jax.random.normal(stream_key, dims, jnp.float32)
    if split:
        drawn = drawn * level_of(stream_key, dims, split, -0.22, 0.18)
    return jnp.clip(drawn, -most, most).astype(dtype)


def setup_inputs(seed: int = 0) -> dict:
    keys = jax.random.split(jax.random.key(seed), 4)
    return {
        "grads": noise(keys[0], (PARAMS, EXAMPLES), 1.0, 6.0, ((0, 8), (1, 4)), jnp.float32),
        "projection": noise(keys[1], (PARAMS, K), 1.0, 6.0, ((0, 8),)),
        "whitener": draw_whitener(jax.random.fold_in(keys[3], 71), 0),
    }


def reference(grads, projection, whitener):
    low_grads = grads.astype(jnp.bfloat16)
    sketch = jnp.dot(projection.T, low_grads, preferred_element_type=jnp.float32) * (1.0 / math.sqrt(PARAMS))
    whitened = jnp.dot(whitener, sketch, precision=lax.Precision.HIGHEST).astype(jnp.bfloat16)
    return jnp.dot(whitened.T, whitened, preferred_element_type=jnp.float32) / K
```

```python
import functools
import math

import jax
import jax.numpy as jnp
from jax import lax
from jax.experimental import pallas as pl
from jax.experimental.pallas import tpu as pltpu
from jax.sharding import PartitionSpec as P

MESH = pl.DeviceIdType.MESH
BF16 = jnp.bfloat16
F32 = jnp.float32
N_CHUNKS = 4
K_BLOCK = 512
K_LATER = 1536


def kernel(
    n_p, n_e, norm,
    g_hbm, proj_hbm, w_hbm, out_ref,
    gbuf, pbuf, gt, acc, own, sbuf, rbuf, wf32, wall, wacc, row, zbuf, col,
    g_sem, p0_sem, p_sem, w_sem,
    rs_send, rs_recv, w_send, w_recv, wf_send, wf_recv,
    row_send, row_recv, rf_send, rf_recv, z_send, z_recv, c_send, c_recv, l_sem,
):
    p = lax.axis_index("param")
    e = lax.axis_index("ex")
    depth, width = g_hbm.shape
    sketch = proj_hbm.shape[1]
    jw = sketch // N_CHUNKS
    piece = width // n_p
    wrows = sketch // n_p
    tile = out_ref.shape[1]
    nk = depth // K_BLOCK
    partner = p + 1 - 2 * (p % 2)

    w_load = pltpu.make_async_copy(w_hbm, wf32, w_sem)
    w_load.start()
    g_loads, p0_loads, p_loads = [], [], []
    for k in range(nk):
        rows = pl.ds(k * K_BLOCK, K_BLOCK)
        c = pltpu.make_async_copy(g_hbm.at[rows, :], gbuf.at[rows, :], g_sem.at[k])
        c.start()
        g_loads.append(c)
        c = pltpu.make_async_copy(
            proj_hbm.at[rows, pl.ds(0, jw)], pbuf.at[0, rows, :], p0_sem.at[k]
        )
        c.start()
        p0_loads.append(c)
    for j in range(1, N_CHUNKS):
        c = pltpu.make_async_copy(
            proj_hbm.at[:, pl.ds(j * jw, jw)], pbuf.at[j], p_sem.at[j]
        )
        c.start()
        p_loads.append(c)

    barrier = pltpu.get_barrier_semaphore()
    for d in range(1, n_p):
        pl.semaphore_signal(
            barrier, inc=1, device_id={"param": (p + d) % n_p}, device_id_type=MESH
        )
    for d in range(1, n_e):
        pl.semaphore_signal(
            barrier, inc=1, device_id={"ex": (e + d) % n_e}, device_id_type=MESH
        )
    w_load.wait()
    wall[pl.ds(pl.multiple_of(p * wrows, wrows), wrows), :] = wf32[...].astype(BF16)
    pl.semaphore_wait(barrier, n_p - 1 + n_e - 1)

    def remote(src, dst, ssem, rsem, to):
        return pltpu.make_async_remote_copy(
            src_ref=src, dst_ref=dst, send_sem=ssem, recv_sem=rsem,
            device_id=to, device_id_type=MESH,
        )

    def w_block(q):
        return wall.at[pl.ds(pl.multiple_of(q * wrows, wrows), wrows), :]

    same = [(p + 2 * d) % n_p for d in range(1, n_p // 2)]
    other = [(partner + 2 * d) % n_p for d in range(1, n_p // 2)]
    w_copies = []
    for d, q in enumerate(same):
        c = remote(w_block(p), w_block(p), w_send.at[d], w_recv.at[p], {"param": q})
        c.start()
        w_copies.append(c)
    c = remote(
        w_block(p), w_block(p), w_send.at[n_p // 2 - 1], w_recv.at[p], {"param": partner}
    )
    c.start()
    w_copies.append(c)

    def forward(block, recv, fsend, frecv, q, d):
        remote(block(q), block(q), fsend.at[d], recv.at[q], {"param": partner}).wait_recv()
        c = remote(block(q), block(q), fsend.at[d], frecv.at[q], {"param": partner})
        c.start()
        return c

    rs_copies = []

    def finish_chunk(j):
        cols = pl.ds(j * jw, jw)
        own[:, cols] = acc[pl.ds(pl.multiple_of(p * piece, piece), piece), :]
        sbuf[:, cols] = acc[...].astype(BF16)
        for d in range(1, n_p):
            q = (p + d) % n_p
            c = remote(
                sbuf.at[pl.ds(pl.multiple_of(q * piece, piece), piece), cols],
                rbuf.at[p, :, cols],
                rs_send.at[j, d],
                rs_recv.at[j, p],
                {"param": q},
            )
            c.start()
            rs_copies.append(c)

    def absorb_chunk(j):
        cols = pl.ds(j * jw, jw)
        total = own[:, cols]
        for d in range(1, n_p):
            q = (p + d) % n_p
            remote(
                sbuf.at[pl.ds(0, piece), cols], rbuf.at[q, :, cols],
                rs_send.at[j, d], rs_recv.at[j, q], {"param": q},
            ).wait_recv()
            total = total + rbuf[q, :, cols].astype(F32)
        total = total * norm
        high = total.astype(BF16)
        low = (total - high.astype(F32)).astype(BF16)
        both = jnp.concatenate([high, low], axis=0)
        part = lax.dot_general(
            both, wall[:, cols], (((1,), (1,)), ((), ())), preferred_element_type=F32
        )
        part = part[:piece] + part[piece:]
        if j == 0:
            wacc[...] = part
        else:
            wacc[...] += part

    acc[...] = jnp.zeros_like(acc)
    for k in range(nk):
        g_loads[k].wait()
        p0_loads[k].wait()

        rows = pl.ds(k * K_BLOCK, K_BLOCK)
        gk = gbuf[rows, :].astype(BF16).T
        gt[:, rows] = gk
        acc[...] += jnp.dot(gk, pbuf[0, rows, :], preferred_element_type=F32)
    finish_chunk(0)
    forwards = []
    for j in range(1, N_CHUNKS):
        p_loads[j - 1].wait()
        acc[...] = jnp.zeros_like(acc)

        @pl.loop(0, depth // K_LATER)
        def _(k):
            rows = pl.ds(pl.multiple_of(k * K_LATER, K_LATER), K_LATER)
            acc[...] += jnp.dot(gt[:, rows], pbuf[j, rows, :], preferred_element_type=F32)

        finish_chunk(j)
        if j == 2:
            for d, q in enumerate(same):
                forwards.append(forward(w_block, w_recv, wf_send, wf_recv, q, d))
    remote(
        w_block(p), w_block(partner), w_send.at[0], w_recv.at[partner], {"param": partner}
    ).wait_recv()
    for d, q in enumerate(other):
        remote(
            w_block(q), w_block(q), wf_send.at[d], wf_recv.at[q], {"param": partner}
        ).wait_recv()
    for j in range(N_CHUNKS):
        absorb_chunk(j)

    def row_block(q):
        return row.at[pl.ds(pl.multiple_of(q * piece, piece), piece), :]

    row[pl.ds(pl.multiple_of(p * piece, piece), piece), :] = wacc[...].astype(BF16)
    out_copies = []
    for d in range(1, n_e):
        c = remote(
            row_block(p), zbuf.at[e], z_send.at[d], z_recv.at[e], {"ex": (e + d) % n_e}
        )
        c.start()
        out_copies.append(c)
    for d, q in enumerate(same):
        c = remote(row_block(p), row_block(p), row_send.at[d], row_recv.at[p], {"param": q})
        c.start()
        out_copies.append(c)
    c = remote(
        row_block(p), row_block(p), row_send.at[n_p // 2 - 1], row_recv.at[p],
        {"param": partner},
    )
    c.start()
    out_copies.append(c)

    def pass_on(src, group, d):
        first = group * width + p * piece
        q = first // tile
        slot = (first % tile) // piece
        dst = col.at[pl.ds(pl.multiple_of(slot * piece, piece), piece), :]
        c = remote(src, dst, c_send.at[d], c_recv.at[slot], {"param": q})
        l = pltpu.make_async_copy(src, dst, l_sem.at[d])

        @pl.when(q != p)
        def _():
            c.start()

        @pl.when(q == p)
        def _():
            l.start()

        return q, c, l

    passed = [pass_on(row_block(p), e, 0)]
    for d in range(1, n_e):
        s = (e + d) % n_e
        remote(
            row_block(p), zbuf.at[s], z_send.at[d], z_recv.at[s], {"ex": s}
        ).wait_recv()
        passed.append(pass_on(zbuf.at[s], s, d))
    for d, q in enumerate(same):
        forwards.append(forward(row_block, row_recv, rf_send, rf_recv, q, d))
    remote(
        row_block(p), row_block(partner), row_send.at[0], row_recv.at[partner],
        {"param": partner},
    ).wait_recv()
    for d, q in enumerate(other):
        remote(
            row_block(q), row_block(q), rf_send.at[d], rf_recv.at[q], {"param": partner}
        ).wait_recv()
    for q, c, l in passed:

        @pl.when(q == p)
        def _(l=l):
            l.wait()

        @pl.when(q != p)
        def _(c=c):
            c.wait_send()

    for slot in range(tile // piece):
        source = ((p * tile) % width) // piece + slot
        dst = col.at[pl.ds(slot * piece, piece), :]

        @pl.when(source != p)
        def _(slot=slot, dst=dst):
            remote(
                row_block(p), dst, c_send.at[0], c_recv.at[slot], {"param": partner}
            ).wait_recv()

    result = lax.dot_general(
        row[...], col[...], (((1,), (1,)), ((), ())), preferred_element_type=F32
    )
    out_ref[...] = result * (1.0 / sketch)

    for c in w_copies + rs_copies + out_copies + forwards:
        c.wait_send()


def solution(mesh):
    n_p, n_e = mesh.shape["param"], mesh.shape["ex"]

    def body(grads, projection, whitener):
        depth, width = grads.shape
        sketch = projection.shape[1]
        piece = width // n_p
        tile = width * n_e // n_p
        jw = sketch // N_CHUNKS
        nk = depth // K_BLOCK
        dma = pltpu.SemaphoreType.DMA
        norm = 1.0 / math.sqrt(depth * n_p)
        half = n_p // 2
        return pl.pallas_call(
            functools.partial(kernel, n_p, n_e, norm),
            out_shape=jax.ShapeDtypeStruct((width, tile), F32),
            in_specs=[pl.BlockSpec(memory_space=pl.ANY)] * 3,
            out_specs=pl.BlockSpec(memory_space=pltpu.VMEM),
            scratch_shapes=[
                pltpu.VMEM((depth, width), F32),
                pltpu.VMEM((N_CHUNKS, depth, jw), BF16),
                pltpu.VMEM((width, depth), BF16),
                pltpu.VMEM((width, jw), F32),
                pltpu.VMEM((piece, sketch), F32),
                pltpu.VMEM((width, sketch), BF16),
                pltpu.VMEM((n_p, piece, sketch), BF16),
                pltpu.VMEM(whitener.shape, F32),
                pltpu.VMEM((sketch, sketch), BF16),
                pltpu.VMEM((piece, sketch), F32),
                pltpu.VMEM((width, sketch), BF16),
                pltpu.VMEM((n_e, piece, sketch), BF16),
                pltpu.VMEM((tile, sketch), BF16),
                dma((nk,)), dma((nk,)), dma((N_CHUNKS,)), dma,
                dma((N_CHUNKS, n_p)), dma((N_CHUNKS, n_p)),
                dma((half,)), dma((n_p,)), dma((half,)), dma((n_p,)),
                dma((half,)), dma((n_p,)), dma((half,)), dma((n_p,)),
                dma((n_e,)), dma((n_e,)), dma((n_e,)), dma((tile // piece,)), dma((n_e,)),
            ],
            compiler_params=pltpu.CompilerParams(
                collective_id=0, has_side_effects=True, vmem_limit_bytes=67043328
            ),
        )(grads, projection, whitener)

    return jax.shard_map(
        body,
        mesh=mesh,
        in_specs=(P("param", "ex"), P("param", None), P("param", None)),
        out_specs=P("ex", "param"),
        check_vma=False,
    )
```

```python
import functools
import math

import jax
import jax.numpy as jnp
from jax import lax
from jax.experimental import pallas as pl
from jax.experimental.pallas import tpu as pltpu
from jax.sharding import PartitionSpec as P

MESH = pl.DeviceIdType.MESH
BF16 = jnp.bfloat16
F32 = jnp.float32
HALVES = 2
K_BLOCK = 512
K_LATER = 1536
B_CHUNKS = (256, 256, 256, 256)


def kernel(
    n_p, n_e, norm,
    g_hbm, proj_hbm, w_hbm, out_ref,
    gbuf, pbuf, gt, acc, keep, xsend, xrecv, sbuf, rbuf, wf32, wall, wacc, row, zbuf, col,
    g_sem, p_sem, w_sem,
    x_send, x_recv, rs_send, rs_recv, w_send, w_recv, wf_send, wf_recv,
    row_send, row_recv, rf_send, rf_recv, z_send, z_recv, c_send, c_recv, l_sem,
):
    p = lax.axis_index("param")
    e = lax.axis_index("ex")
    depth, width = g_hbm.shape
    sketch = proj_hbm.shape[1]
    hw = width // HALVES
    piece = hw // n_p
    wrows = sketch // n_p
    tile = out_ref.shape[1]
    nk = depth // K_BLOCK
    chips = n_p // 2
    chip, core = p // 2, p % 2
    partner = p + 1 - 2 * core

    w_load = pltpu.make_async_copy(w_hbm, wf32, w_sem)
    w_load.start()
    g_loads, p_loads = [], []
    for h in range(HALVES):
        for k in range(nk):
            rows = pl.ds(k * K_BLOCK, K_BLOCK)
            c = pltpu.make_async_copy(
                g_hbm.at[rows, pl.ds(h * hw, hw)], gbuf.at[h, rows, :], g_sem.at[h, k]
            )
            c.start()
            g_loads.append(c)
            if h == 0:
                c = pltpu.make_async_copy(
                    proj_hbm.at[rows, :], pbuf.at[rows, :], p_sem.at[k]
                )
                c.start()
                p_loads.append(c)

    barrier = pltpu.get_barrier_semaphore()
    for d in range(1, n_p):
        pl.semaphore_signal(
            barrier, inc=1, device_id={"param": (p + d) % n_p}, device_id_type=MESH
        )
    for d in range(1, n_e):
        pl.semaphore_signal(
            barrier, inc=1, device_id={"ex": (e + d) % n_e}, device_id_type=MESH
        )
    w_load.wait()
    wall[pl.ds(pl.multiple_of(p * wrows, wrows), wrows), :] = wf32[...].astype(BF16)
    pl.semaphore_wait(barrier, n_p - 1 + n_e - 1)

    def remote(src, dst, ssem, rsem, to):
        return pltpu.make_async_remote_copy(
            src_ref=src, dst_ref=dst, send_sem=ssem, recv_sem=rsem,
            device_id=to, device_id_type=MESH,
        )

    started = []

    def send(*args):
        c = remote(*args)
        c.start()
        started.append(c)

    def w_block(q):
        return wall.at[pl.ds(pl.multiple_of(q * wrows, wrows), wrows), :]

    same = [(p + 2 * d) % n_p for d in range(1, chips)]
    other = [(partner + 2 * d) % n_p for d in range(1, chips)]
    for d, q in enumerate(same):
        send(w_block(p), w_block(p), w_send.at[d], w_recv.at[p], {"param": q})
    send(w_block(p), w_block(p), w_send.at[chips - 1], w_recv.at[p], {"param": partner})

    def forward_w():
        for d, q in enumerate(same):
            remote(
                w_block(q), w_block(q), wf_send.at[d], w_recv.at[q], {"param": q}
            ).wait_recv()
            send(w_block(q), w_block(q), wf_send.at[d], wf_recv.at[q], {"param": partner})

    def await_w():
        remote(
            w_block(p), w_block(partner), w_send.at[0], w_recv.at[partner],
            {"param": partner},
        ).wait_recv()
        for d, q in enumerate(other):
            remote(
                w_block(q), w_block(q), wf_send.at[d], wf_recv.at[q], {"param": partner}
            ).wait_recv()

    def exchange(h, i, first, size):
        cols = pl.ds(first, size)
        for c in range(chips):
            rows = pl.ds(c * piece, piece)
            mine = pl.ds(pl.multiple_of((2 * c + core) * piece, piece), piece)
            theirs = pl.ds(pl.multiple_of((2 * c + 1 - core) * piece, piece), piece)
            keep[h, rows, cols] = acc[mine, pl.ds(0, size)]
            xsend[h, rows, cols] = acc[theirs, pl.ds(0, size)]
        send(
            xsend.at[h, :, cols], xrecv.at[h, :, cols], x_send.at[h, i], x_recv.at[h, i],
            {"param": partner},
        )

    def scatter(h, i, first, size):
        cols = pl.ds(first, size)
        remote(
            xsend.at[h, :, cols], xrecv.at[h, :, cols], x_send.at[h, i], x_recv.at[h, i],
            {"param": partner},
        ).wait_recv()
        both = keep[h, :, cols] + xrecv[h, :, cols]
        keep[h, :, cols] = both
        sbuf[h, :, cols] = both.astype(BF16)
        for d in range(1, chips):
            to = (chip + d) % chips
            send(
                sbuf.at[h, pl.ds(pl.multiple_of(to * piece, piece), piece), cols],
                rbuf.at[h, chip, :, cols],
                rs_send.at[h, i, d],
                rs_recv.at[h, i, chip],
                {"param": 2 * to + core},
            )

    def absorb(h, i, first, size):
        cols = pl.ds(first, size)
        total = keep[h, pl.ds(pl.multiple_of(chip * piece, piece), piece), cols]
        for d in range(1, chips):
            a = (chip + d) % chips
            remote(
                sbuf.at[h, pl.ds(0, piece), cols], rbuf.at[h, a, :, cols],
                rs_send.at[h, i, d], rs_recv.at[h, i, a], {"param": 2 * a + core},
            ).wait_recv()
            total = total + rbuf[h, a, :, cols].astype(F32)
        total = total * norm
        high = total.astype(BF16)
        low = (total - high.astype(F32)).astype(BF16)
        stacked = jnp.concatenate([high, low], axis=0)
        part = lax.dot_general(
            stacked, wall[:, cols], (((1,), (1,)), ((), ())), preferred_element_type=F32
        )
        part = part[:piece] + part[piece:]
        if i == 0:
            wacc[h] = part
        else:
            wacc[h] = wacc[h] + part

    def row_block(h, q):
        return row.at[h, pl.ds(pl.multiple_of(q * piece, piece), piece), :]

    def spread(h):
        row[h, pl.ds(pl.multiple_of(p * piece, piece), piece), :] = wacc[h].astype(BF16)
        mine = row_block(h, p)
        for d in range(1, n_e):
            send(mine, zbuf.at[h, e], z_send.at[h, d], z_recv.at[h, e], {"ex": (e + d) % n_e})
        for d, q in enumerate(same):
            send(mine, mine, row_send.at[h, d], row_recv.at[h, p], {"param": q})
        send(mine, mine, row_send.at[h, chips - 1], row_recv.at[h, p], {"param": partner})
        pass_on(h, mine, e, 0)

    passed = []

    def pass_on(h, src, group, d):
        first = group * width + h * hw + p * piece
        q = first // tile
        slot = (first % tile) // piece
        dst = col.at[pl.ds(pl.multiple_of(slot * piece, piece), piece), :]
        c = remote(src, dst, c_send.at[h, d], c_recv.at[slot], {"param": q})
        l = pltpu.make_async_copy(src, dst, l_sem.at[h, d])

        @pl.when(q != p)
        def _():
            c.start()

        @pl.when(q == p)
        def _():
            l.start()

        passed.append((q, c, l))

    def pass_all(h):
        for d in range(1, n_e):
            s = (e + d) % n_e
            remote(
                row_block(h, p), zbuf.at[h, s], z_send.at[h, d], z_recv.at[h, s], {"ex": s}
            ).wait_recv()
            pass_on(h, zbuf.at[h, s], s, d)

    def forward_rows(h):
        for d, q in enumerate(same):
            block = row_block(h, q)
            remote(block, block, rf_send.at[h, d], row_recv.at[h, q], {"param": q}).wait_recv()
            send(block, block, rf_send.at[h, d], rf_recv.at[h, q], {"param": partner})

    def await_rows(h):
        block = row_block(h, partner)
        remote(
            block, block, row_send.at[h, 0], row_recv.at[h, partner], {"param": partner}
        ).wait_recv()
        for d, q in enumerate(other):
            block = row_block(h, q)
            remote(
                block, block, rf_send.at[h, d], rf_recv.at[h, q], {"param": partner}
            ).wait_recv()

    for k in range(nk):
        rows = pl.ds(k * K_BLOCK, K_BLOCK)
        g_loads[k].wait()
        p_loads[k].wait()
        part = jnp.dot(
            gbuf[0, rows, :].astype(BF16).T, pbuf[rows, :], preferred_element_type=F32
        )
        if k == 0:
            acc[...] = part
        else:
            acc[...] += part
    exchange(0, 0, 0, sketch)

    first = 0
    spans = []
    for i, size in enumerate(B_CHUNKS):
        cols = pl.ds(first, size)
        here = pl.ds(0, size)
        if i == 0:
            for k in range(nk):
                rows = pl.ds(k * K_BLOCK, K_BLOCK)
                g_loads[nk + k].wait()
                gk = gbuf[1, rows, :].astype(BF16).T
                gt[:, rows] = gk
                part = jnp.dot(gk, pbuf[rows, cols], preferred_element_type=F32)
                if k == 0:
                    acc[:, here] = part
                else:
                    acc[:, here] += part
        else:
            acc[:, here] = jnp.zeros((hw, size), F32)

            @pl.loop(0, depth // K_LATER)
            def _(k):
                rows = pl.ds(pl.multiple_of(k * K_LATER, K_LATER), K_LATER)
                acc[:, here] += jnp.dot(
                    gt[:, rows], pbuf[rows, cols], preferred_element_type=F32
                )

        exchange(1, i, first, size)
        if i == 0:
            scatter(0, 0, 0, sketch)
            forward_w()
        else:
            scatter(1, i - 1, *spans[-1])
        if i == 2:
            await_w()
            absorb(0, 0, 0, sketch)
            spread(0)
        spans.append((first, size))
        first += size
    last = len(spans) - 1
    scatter(1, last, *spans[last])
    forward_rows(0)
    for i in range(last):
        absorb(1, i, *spans[i])
    pass_all(0)
    absorb(1, last, *spans[last])
    spread(1)
    await_rows(0)
    forward_rows(1)
    pass_all(1)
    for q, c, l in passed:

        @pl.when(q == p)
        def _(l=l):
            l.wait()

        @pl.when(q != p)
        def _(c=c):
            c.wait_send()

    for slot in range(tile // piece):
        source = ((p * tile) % hw) // piece + slot
        dst = col.at[pl.ds(slot * piece, piece), :]

        @pl.when(source % n_p != p)
        def _(slot=slot, dst=dst):
            remote(
                row_block(0, p), dst, c_send.at[0, 0], c_recv.at[slot], {"param": partner}
            ).wait_recv()

    def product(h):
        out_ref[pl.ds(h * hw, hw), :] = lax.dot_general(
            row[h], col[...], (((1,), (1,)), ((), ())), preferred_element_type=F32
        ) * (1.0 / sketch)

    product(0)
    await_rows(1)
    product(1)
    for c in started:
        c.wait_send()


def solution(mesh):
    n_p, n_e = mesh.shape["param"], mesh.shape["ex"]

    def body(grads, projection, whitener):
        depth, width = grads.shape
        sketch = projection.shape[1]
        hw = width // HALVES
        piece = hw // n_p
        tile = width * n_e // n_p
        nk = depth // K_BLOCK
        dma = pltpu.SemaphoreType.DMA
        norm = 1.0 / math.sqrt(depth * n_p)
        chips = n_p // 2
        steps = len(B_CHUNKS)
        return pl.pallas_call(
            functools.partial(kernel, n_p, n_e, norm),
            out_shape=jax.ShapeDtypeStruct((width, tile), F32),
            in_specs=[pl.BlockSpec(memory_space=pl.ANY)] * 3,
            out_specs=pl.BlockSpec(memory_space=pltpu.VMEM),
            scratch_shapes=[
                pltpu.VMEM((HALVES, depth, hw), F32),
                pltpu.VMEM((depth, sketch), BF16),
                pltpu.VMEM((hw, depth), BF16),
                pltpu.VMEM((hw, sketch), F32),
                pltpu.VMEM((HALVES, hw // 2, sketch), F32),
                pltpu.VMEM((HALVES, hw // 2, sketch), F32),
                pltpu.VMEM((HALVES, hw // 2, sketch), F32),
                pltpu.VMEM((HALVES, hw // 2, sketch), BF16),
                pltpu.VMEM((HALVES, chips, piece, sketch), BF16),
                pltpu.VMEM(whitener.shape, F32),
                pltpu.VMEM((sketch, sketch), BF16),
                pltpu.VMEM((HALVES, piece, sketch), F32),
                pltpu.VMEM((HALVES, hw, sketch), BF16),
                pltpu.VMEM((HALVES, n_e, piece, sketch), BF16),
                pltpu.VMEM((tile, sketch), BF16),
                dma((HALVES, nk)), dma((nk,)), dma,
                dma((HALVES, steps)), dma((HALVES, steps)),
                dma((HALVES, steps, chips)), dma((HALVES, steps, chips)),
                dma((chips,)), dma((n_p,)), dma((chips,)), dma((n_p,)),
                dma((HALVES, chips)), dma((HALVES, n_p)),
                dma((HALVES, chips)), dma((HALVES, n_p)),
                dma((HALVES, n_e)), dma((HALVES, n_e)),
                dma((HALVES, n_e)), dma((tile // piece,)), dma((HALVES, n_e)),
            ],
            compiler_params=pltpu.CompilerParams(
                collective_id=0, has_side_effects=True, vmem_limit_bytes=67043328
            ),
        )(grads, projection, whitener)

    return jax.shard_map(
        body,
        mesh=mesh,
        in_specs=(P("param", "ex"), P("param", None), P("param", None)),
        out_specs=P("ex", "param"),
        check_vma=False,
    )
```

```python
import functools
import math

import jax
import jax.numpy as jnp
from jax import lax
from jax.experimental import pallas as pl
from jax.experimental.pallas import tpu as pltpu
from jax.sharding import PartitionSpec as P

MESH = pl.DeviceIdType.MESH
BF16 = jnp.bfloat16
F32 = jnp.float32
HALVES = 2
K_BLOCK = 512
K_LATER = 1536
ENTER_AT = 1
B_CHUNKS = (256, 256, 256, 256)


def kernel(
    n_p, n_e, norm,
    g_hbm, proj_hbm, w_hbm, out_ref,
    gbuf, pbuf, gt, acc, keep, xsend, xrecv, sbuf, rbuf, wf32, wall, wacc, row, zbuf, col,
    g_sem, p_sem, w_sem,
    x_send, x_recv, rs_send, rs_recv, w_send, w_recv, wf_send, wf_recv,
    row_send, row_recv, rf_send, rf_recv, z_send, z_recv, c_send, c_recv, l_sem,
):
    p = lax.axis_index("param")
    e = lax.axis_index("ex")
    depth, width = g_hbm.shape
    sketch = proj_hbm.shape[1]
    hw = width // HALVES
    piece = hw // n_p
    wrows = sketch // n_p
    tile = out_ref.shape[1]
    nk = depth // K_BLOCK
    chips = n_p // 2
    chip, core = p // 2, p % 2
    partner = p + 1 - 2 * core

    w_load = pltpu.make_async_copy(w_hbm, wf32, w_sem)
    w_load.start()
    g_loads, p_loads = [], []
    for h in range(HALVES):
        for k in range(nk):
            rows = pl.ds(k * K_BLOCK, K_BLOCK)
            c = pltpu.make_async_copy(
                g_hbm.at[rows, pl.ds(h * hw, hw)], gbuf.at[h, rows, :], g_sem.at[h, k]
            )
            c.start()
            g_loads.append(c)
            if h == 0:
                c = pltpu.make_async_copy(
                    proj_hbm.at[rows, :], pbuf.at[rows, :], p_sem.at[k]
                )
                c.start()
                p_loads.append(c)

    barrier = pltpu.get_barrier_semaphore()
    for d in range(1, n_p):
        pl.semaphore_signal(
            barrier, inc=1, device_id={"param": (p + d) % n_p}, device_id_type=MESH
        )
    for d in range(1, n_e):
        pl.semaphore_signal(
            barrier, inc=1, device_id={"ex": (e + d) % n_e}, device_id_type=MESH
        )
    def remote(src, dst, ssem, rsem, to):
        return pltpu.make_async_remote_copy(
            src_ref=src, dst_ref=dst, send_sem=ssem, recv_sem=rsem,
            device_id=to, device_id_type=MESH,
        )

    started = []

    def send(*args):
        c = remote(*args)
        c.start()
        started.append(c)

    def w_block(q):
        return wall.at[pl.ds(pl.multiple_of(q * wrows, wrows), wrows), :]

    same = [(p + 2 * d) % n_p for d in range(1, chips)]
    other = [(partner + 2 * d) % n_p for d in range(1, chips)]
    def enter():
        w_load.wait()
        wall[pl.ds(pl.multiple_of(p * wrows, wrows), wrows), :] = wf32[...].astype(BF16)
        pl.semaphore_wait(barrier, n_p - 1 + n_e - 1)
        for d, q in enumerate(same):
            send(w_block(p), w_block(p), w_send.at[d], w_recv.at[p], {"param": q})
        send(w_block(p), w_block(p), w_send.at[chips - 1], w_recv.at[p], {"param": partner})

    def forward_w():
        for d, q in enumerate(same):
            remote(
                w_block(q), w_block(q), wf_send.at[d], w_recv.at[q], {"param": q}
            ).wait_recv()
            send(w_block(q), w_block(q), wf_send.at[d], wf_recv.at[q], {"param": partner})

    def await_w():
        remote(
            w_block(p), w_block(partner), w_send.at[0], w_recv.at[partner],
            {"param": partner},
        ).wait_recv()
        for d, q in enumerate(other):
            remote(
                w_block(q), w_block(q), wf_send.at[d], wf_recv.at[q], {"param": partner}
            ).wait_recv()

    def exchange(h, i, first, size):
        cols = pl.ds(first, size)
        for c in range(chips):
            rows = pl.ds(c * piece, piece)
            mine = pl.ds(pl.multiple_of((2 * c + core) * piece, piece), piece)
            theirs = pl.ds(pl.multiple_of((2 * c + 1 - core) * piece, piece), piece)
            keep[h, rows, cols] = acc[mine, pl.ds(0, size)]
            xsend[h, rows, cols] = acc[theirs, pl.ds(0, size)]
        send(
            xsend.at[h, :, cols], xrecv.at[h, :, cols], x_send.at[h, i], x_recv.at[h, i],
            {"param": partner},
        )

    def scatter(h, i, first, size):
        cols = pl.ds(first, size)
        remote(
            xsend.at[h, :, cols], xrecv.at[h, :, cols], x_send.at[h, i], x_recv.at[h, i],
            {"param": partner},
        ).wait_recv()
        both = keep[h, :, cols] + xrecv[h, :, cols]
        keep[h, :, cols] = both
        sbuf[h, :, cols] = both.astype(BF16)
        for d in range(1, chips):
            to = (chip + d) % chips
            send(
                sbuf.at[h, pl.ds(pl.multiple_of(to * piece, piece), piece), cols],
                rbuf.at[h, chip, :, cols],
                rs_send.at[h, i, d],
                rs_recv.at[h, i, chip],
                {"param": 2 * to + core},
            )

    def absorb(h, i, first, size):
        cols = pl.ds(first, size)
        total = keep[h, pl.ds(pl.multiple_of(chip * piece, piece), piece), cols]
        for d in range(1, chips):
            a = (chip + d) % chips
            remote(
                sbuf.at[h, pl.ds(0, piece), cols], rbuf.at[h, a, :, cols],
                rs_send.at[h, i, d], rs_recv.at[h, i, a], {"param": 2 * a + core},
            ).wait_recv()
            total = total + rbuf[h, a, :, cols].astype(F32)
        total = total * norm
        high = total.astype(BF16)
        low = (total - high.astype(F32)).astype(BF16)
        stacked = jnp.concatenate([high, low], axis=0)
        part = lax.dot_general(
            stacked, wall[:, cols], (((1,), (1,)), ((), ())), preferred_element_type=F32
        )
        part = part[:piece] + part[piece:]
        if i == 0:
            wacc[h] = part
        else:
            wacc[h] = wacc[h] + part

    def row_block(h, q):
        return row.at[h, pl.ds(pl.multiple_of(q * piece, piece), piece), :]

    def spread(h):
        row[h, pl.ds(pl.multiple_of(p * piece, piece), piece), :] = wacc[h].astype(BF16)
        mine = row_block(h, p)
        for d in range(1, n_e):
            send(mine, zbuf.at[h, e], z_send.at[h, d], z_recv.at[h, e], {"ex": (e + d) % n_e})
        for d, q in enumerate(same):
            send(mine, mine, row_send.at[h, d], row_recv.at[h, p], {"param": q})
        send(mine, mine, row_send.at[h, chips - 1], row_recv.at[h, p], {"param": partner})
        pass_on(h, mine, e, 0)

    passed = []

    def pass_on(h, src, group, d):
        first = group * width + h * hw + p * piece
        q = first // tile
        slot = (first % tile) // piece
        dst = col.at[pl.ds(pl.multiple_of(slot * piece, piece), piece), :]
        c = remote(src, dst, c_send.at[h, d], c_recv.at[slot], {"param": q})
        l = pltpu.make_async_copy(src, dst, l_sem.at[h, d])

        @pl.when(q != p)
        def _():
            c.start()

        @pl.when(q == p)
        def _():
            l.start()

        passed.append((q, c, l))

    def pass_all(h):
        for d in range(1, n_e):
            s = (e + n_e - d) % n_e
            remote(
                row_block(h, p), zbuf.at[h, s], z_send.at[h, d], z_recv.at[h, s], {"ex": s}
            ).wait_recv()
            pass_on(h, zbuf.at[h, s], s, d)

    def forward_rows(h):
        for d, q in enumerate(same):
            block = row_block(h, q)
            remote(block, block, rf_send.at[h, d], row_recv.at[h, q], {"param": q}).wait_recv()
            send(block, block, rf_send.at[h, d], rf_recv.at[h, q], {"param": partner})

    def await_rows(h):
        block = row_block(h, partner)
        remote(
            block, block, row_send.at[h, 0], row_recv.at[h, partner], {"param": partner}
        ).wait_recv()
        for d, q in enumerate(other):
            block = row_block(h, q)
            remote(
                block, block, rf_send.at[h, d], rf_recv.at[h, q], {"param": partner}
            ).wait_recv()

    for k in range(nk):
        rows = pl.ds(k * K_BLOCK, K_BLOCK)
        g_loads[k].wait()
        p_loads[k].wait()
        part = jnp.dot(
            gbuf[0, rows, :].astype(BF16).T, pbuf[rows, :], preferred_element_type=F32
        )
        if k == 0:
            acc[...] = part
        else:
            acc[...] += part
        if k == ENTER_AT:
            enter()
    exchange(0, 0, 0, sketch)

    first = 0
    spans = []
    for i, size in enumerate(B_CHUNKS):
        cols = pl.ds(first, size)
        here = pl.ds(0, size)
        if i == 0:
            for k in range(nk):
                rows = pl.ds(k * K_BLOCK, K_BLOCK)
                g_loads[nk + k].wait()
                gk = gbuf[1, rows, :].astype(BF16).T
                gt[:, rows] = gk
                part = jnp.dot(gk, pbuf[rows, cols], preferred_element_type=F32)
                if k == 0:
                    acc[:, here] = part
                else:
                    acc[:, here] += part
                if k == nk // 2:
                    scatter(0, 0, 0, sketch)
        else:
            acc[:, here] = jnp.zeros((hw, size), F32)

            @pl.loop(0, depth // K_LATER)
            def _(k):
                rows = pl.ds(pl.multiple_of(k * K_LATER, K_LATER), K_LATER)
                acc[:, here] += jnp.dot(
                    gt[:, rows], pbuf[rows, cols], preferred_element_type=F32
                )

        exchange(1, i, first, size)
        if i > 0:
            scatter(1, i - 1, *spans[-1])
        if i == 2:
            forward_w()
        if i == 3:
            await_w()
            absorb(0, 0, 0, sketch)
            spread(0)
        spans.append((first, size))
        first += size
    last = len(spans) - 1
    scatter(1, last, *spans[last])
    forward_rows(0)
    for i in range(last):
        absorb(1, i, *spans[i])
    pass_all(0)
    absorb(1, last, *spans[last])
    spread(1)
    pass_all(1)
    await_rows(0)
    forward_rows(1)
    for q, c, l in passed:

        @pl.when(q == p)
        def _(l=l):
            l.wait()

        @pl.when(q != p)
        def _(c=c):
            c.wait_send()

    for slot in range(tile // piece):
        source = ((p * tile) % hw) // piece + slot
        dst = col.at[pl.ds(slot * piece, piece), :]

        @pl.when(source % n_p != p)
        def _(slot=slot, dst=dst):
            remote(
                row_block(0, p), dst, c_send.at[0, 0], c_recv.at[slot], {"param": partner}
            ).wait_recv()

    def product(h):
        out_ref[pl.ds(h * hw, hw), :] = lax.dot_general(
            row[h], col[...], (((1,), (1,)), ((), ())), preferred_element_type=F32
        ) * (1.0 / sketch)

    product(0)
    await_rows(1)
    product(1)
    for c in started:
        c.wait_send()


def solution(mesh):
    n_p, n_e = mesh.shape["param"], mesh.shape["ex"]

    def body(grads, projection, whitener):
        depth, width = grads.shape
        sketch = projection.shape[1]
        hw = width // HALVES
        piece = hw // n_p
        tile = width * n_e // n_p
        nk = depth // K_BLOCK
        dma = pltpu.SemaphoreType.DMA
        norm = 1.0 / math.sqrt(depth * n_p)
        chips = n_p // 2
        steps = len(B_CHUNKS)
        return pl.pallas_call(
            functools.partial(kernel, n_p, n_e, norm),
            out_shape=jax.ShapeDtypeStruct((width, tile), F32),
            in_specs=[pl.BlockSpec(memory_space=pl.ANY)] * 3,
            out_specs=pl.BlockSpec(memory_space=pltpu.VMEM),
            scratch_shapes=[
                pltpu.VMEM((HALVES, depth, hw), F32),
                pltpu.VMEM((depth, sketch), BF16),
                pltpu.VMEM((hw, depth), BF16),
                pltpu.VMEM((hw, sketch), F32),
                pltpu.VMEM((HALVES, hw // 2, sketch), F32),
                pltpu.VMEM((HALVES, hw // 2, sketch), F32),
                pltpu.VMEM((HALVES, hw // 2, sketch), F32),
                pltpu.VMEM((HALVES, hw // 2, sketch), BF16),
                pltpu.VMEM((HALVES, chips, piece, sketch), BF16),
                pltpu.VMEM(whitener.shape, F32),
                pltpu.VMEM((sketch, sketch), BF16),
                pltpu.VMEM((HALVES, piece, sketch), F32),
                pltpu.VMEM((HALVES, hw, sketch), BF16),
                pltpu.VMEM((HALVES, n_e, piece, sketch), BF16),
                pltpu.VMEM((tile, sketch), BF16),
                dma((HALVES, nk)), dma((nk,)), dma,
                dma((HALVES, steps)), dma((HALVES, steps)),
                dma((HALVES, steps, chips)), dma((HALVES, steps, chips)),
                dma((chips,)), dma((n_p,)), dma((chips,)), dma((n_p,)),
                dma((HALVES, chips)), dma((HALVES, n_p)),
                dma((HALVES, chips)), dma((HALVES, n_p)),
                dma((HALVES, n_e)), dma((HALVES, n_e)),
                dma((HALVES, n_e)), dma((tile // piece,)), dma((HALVES, n_e)),
            ],
            compiler_params=pltpu.CompilerParams(
                collective_id=0, has_side_effects=True, vmem_limit_bytes=67043328
            ),
        )(grads, projection, whitener)

    return jax.shard_map(
        body,
        mesh=mesh,
        in_specs=(P("param", "ex"), P("param", None), P("param", None)),
        out_specs=P("ex", "param"),
        check_vma=False,
    )
```

```python
import functools
import math

import jax
import jax.numpy as jnp
from jax import lax
from jax.experimental import pallas as pl
from jax.experimental.pallas import tpu as pltpu
from jax.sharding import PartitionSpec as P

MESH = pl.DeviceIdType.MESH
BF16 = jnp.bfloat16
F32 = jnp.float32
HALVES = 2
K_BLOCK = 512
K_LATER = 1536
ENTER_AT = 0
B_CHUNKS = (256, 256, 256, 256)


def kernel(
    n_p, n_e, norm,
    g_hbm, proj_hbm, w_hbm, out_ref,
    gbuf, pbuf, gt, acc, keep, xsend, xrecv, sbuf, rbuf, wf32, wall, wacc, row, zbuf, col,
    g_sem, p_sem, w_sem,
    x_send, x_recv, rs_send, rs_recv, w_send, w_recv, wf_send, wf_recv,
    row_send, row_recv, rf_send, rf_recv, z_send, z_recv, c_send, c_recv, l_sem,
):
    p = lax.axis_index("param")
    e = lax.axis_index("ex")
    depth, width = g_hbm.shape
    sketch = proj_hbm.shape[1]
    hw = width // HALVES
    piece = hw // n_p
    wrows = sketch // n_p
    tile = out_ref.shape[1]
    nk = depth // K_BLOCK
    chips = n_p // 2
    chip, core = p // 2, p % 2
    partner = p + 1 - 2 * core

    w_load = pltpu.make_async_copy(w_hbm, wf32, w_sem)
    w_load.start()
    g_loads, p_loads = [], []
    for h in range(HALVES):
        for k in range(nk):
            rows = pl.ds(k * K_BLOCK, K_BLOCK)
            c = pltpu.make_async_copy(
                g_hbm.at[rows, pl.ds(h * hw, hw)], gbuf.at[h, rows, :], g_sem.at[h, k]
            )
            c.start()
            g_loads.append(c)
            if h == 0:
                c = pltpu.make_async_copy(
                    proj_hbm.at[rows, :], pbuf.at[rows, :], p_sem.at[k]
                )
                c.start()
                p_loads.append(c)

    barrier = pltpu.get_barrier_semaphore()
    for d in range(1, n_p):
        pl.semaphore_signal(
            barrier, inc=1, device_id={"param": (p + d) % n_p}, device_id_type=MESH
        )
    for d in range(1, n_e):
        pl.semaphore_signal(
            barrier, inc=1, device_id={"ex": (e + d) % n_e}, device_id_type=MESH
        )
    def remote(src, dst, ssem, rsem, to):
        return pltpu.make_async_remote_copy(
            src_ref=src, dst_ref=dst, send_sem=ssem, recv_sem=rsem,
            device_id=to, device_id_type=MESH,
        )

    started = []

    def send(*args):
        c = remote(*args)
        c.start()
        started.append(c)

    def w_block(q):
        return wall.at[pl.ds(pl.multiple_of(q * wrows, wrows), wrows), :]

    same = [(p + 2 * d) % n_p for d in range(1, chips)]
    other = [(partner + 2 * d) % n_p for d in range(1, chips)]
    def enter():
        w_load.wait()
        wall[pl.ds(pl.multiple_of(p * wrows, wrows), wrows), :] = wf32[...].astype(BF16)
        pl.semaphore_wait(barrier, n_p - 1 + n_e - 1)
        for d, q in enumerate(same):
            send(w_block(p), w_block(p), w_send.at[d], w_recv.at[p], {"param": q})
        send(w_block(p), w_block(p), w_send.at[chips - 1], w_recv.at[p], {"param": partner})

    def forward_w():
        for d, q in enumerate(same):
            remote(
                w_block(q), w_block(q), wf_send.at[d], w_recv.at[q], {"param": q}
            ).wait_recv()
            send(w_block(q), w_block(q), wf_send.at[d], wf_recv.at[q], {"param": partner})

    def await_w():
        remote(
            w_block(p), w_block(partner), w_send.at[0], w_recv.at[partner],
            {"param": partner},
        ).wait_recv()
        for d, q in enumerate(other):
            remote(
                w_block(q), w_block(q), wf_send.at[d], wf_recv.at[q], {"param": partner}
            ).wait_recv()

    def exchange(h, i, first, size):
        cols = pl.ds(first, size)
        for c in range(chips):
            rows = pl.ds(c * piece, piece)
            mine = pl.ds(pl.multiple_of((2 * c + core) * piece, piece), piece)
            theirs = pl.ds(pl.multiple_of((2 * c + 1 - core) * piece, piece), piece)
            keep[h, rows, cols] = acc[mine, pl.ds(0, size)]
            xsend[h, rows, cols] = acc[theirs, pl.ds(0, size)]
        send(
            xsend.at[h, :, cols], xrecv.at[h, :, cols], x_send.at[h, i], x_recv.at[h, i],
            {"param": partner},
        )

    def scatter(h, i, first, size):
        cols = pl.ds(first, size)
        remote(
            xsend.at[h, :, cols], xrecv.at[h, :, cols], x_send.at[h, i], x_recv.at[h, i],
            {"param": partner},
        ).wait_recv()
        both = keep[h, :, cols] + xrecv[h, :, cols]
        keep[h, :, cols] = both
        sbuf[h, :, cols] = both.astype(BF16)
        for d in range(1, chips):
            to = (chip + d) % chips
            send(
                sbuf.at[h, pl.ds(pl.multiple_of(to * piece, piece), piece), cols],
                rbuf.at[h, chip, :, cols],
                rs_send.at[h, i, d],
                rs_recv.at[h, i, chip],
                {"param": 2 * to + core},
            )

    def absorb(h, i, first, size):
        cols = pl.ds(first, size)
        total = keep[h, pl.ds(pl.multiple_of(chip * piece, piece), piece), cols]
        for d in range(1, chips):
            a = (chip + d) % chips
            remote(
                sbuf.at[h, pl.ds(0, piece), cols], rbuf.at[h, a, :, cols],
                rs_send.at[h, i, d], rs_recv.at[h, i, a], {"param": 2 * a + core},
            ).wait_recv()
            total = total + rbuf[h, a, :, cols].astype(F32)
        total = total * norm
        high = total.astype(BF16)
        low = (total - high.astype(F32)).astype(BF16)
        stacked = jnp.concatenate([high, low], axis=0)
        part = lax.dot_general(
            stacked, wall[:, cols], (((1,), (1,)), ((), ())), preferred_element_type=F32
        )
        part = part[:piece] + part[piece:]
        if i == 0:
            wacc[h] = part
        else:
            wacc[h] = wacc[h] + part

    def row_block(h, q):
        return row.at[h, pl.ds(pl.multiple_of(q * piece, piece), piece), :]

    def spread(h):
        row[h, pl.ds(pl.multiple_of(p * piece, piece), piece), :] = wacc[h].astype(BF16)
        mine = row_block(h, p)
        for d in range(1, n_e):
            send(mine, zbuf.at[h, e], z_send.at[h, d], z_recv.at[h, e], {"ex": (e + d) % n_e})
        for d, q in enumerate(same):
            send(mine, mine, row_send.at[h, d], row_recv.at[h, p], {"param": q})
        send(mine, mine, row_send.at[h, chips - 1], row_recv.at[h, p], {"param": partner})
        pass_on(h, mine, e, 0)

    passed = []

    def pass_on(h, src, group, d):
        first = group * width + h * hw + p * piece
        q = first // tile
        slot = (first % tile) // piece
        dst = col.at[pl.ds(pl.multiple_of(slot * piece, piece), piece), :]
        c = remote(src, dst, c_send.at[h, d], c_recv.at[slot], {"param": q})
        l = pltpu.make_async_copy(src, dst, l_sem.at[h, d])

        @pl.when(q != p)
        def _():
            c.start()

        @pl.when(q == p)
        def _():
            l.start()

        passed.append((q, c, l))

    def pass_all(h):
        for d in range(1, n_e):
            s = (e + n_e - d) % n_e
            remote(
                row_block(h, p), zbuf.at[h, s], z_send.at[h, d], z_recv.at[h, s], {"ex": s}
            ).wait_recv()
            pass_on(h, zbuf.at[h, s], s, d)

    def forward_rows(h):
        for d, q in enumerate(same):
            block = row_block(h, q)
            remote(block, block, rf_send.at[h, d], row_recv.at[h, q], {"param": q}).wait_recv()
            send(block, block, rf_send.at[h, d], rf_recv.at[h, q], {"param": partner})

    def await_rows(h):
        block = row_block(h, partner)
        remote(
            block, block, row_send.at[h, 0], row_recv.at[h, partner], {"param": partner}
        ).wait_recv()
        for d, q in enumerate(other):
            block = row_block(h, q)
            remote(
                block, block, rf_send.at[h, d], rf_recv.at[h, q], {"param": partner}
            ).wait_recv()

    for k in range(nk):
        rows = pl.ds(k * K_BLOCK, K_BLOCK)
        g_loads[k].wait()
        p_loads[k].wait()
        part = jnp.dot(
            gbuf[0, rows, :].astype(BF16).T, pbuf[rows, :], preferred_element_type=F32
        )
        if k == 0:
            acc[...] = part
        else:
            acc[...] += part
        if k == ENTER_AT:
            enter()
    exchange(0, 0, 0, sketch)

    first = 0
    spans = []
    for i, size in enumerate(B_CHUNKS):
        cols = pl.ds(first, size)
        here = pl.ds(0, size)
        if i == 0:
            for k in range(nk):
                rows = pl.ds(k * K_BLOCK, K_BLOCK)
                g_loads[nk + k].wait()
                gk = gbuf[1, rows, :].astype(BF16).T
                gt[:, rows] = gk
                part = jnp.dot(gk, pbuf[rows, cols], preferred_element_type=F32)
                if k == 0:
                    acc[:, here] = part
                else:
                    acc[:, here] += part
                if k == nk // 2:
                    scatter(0, 0, 0, sketch)
        else:
            acc[:, here] = jnp.zeros((hw, size), F32)

            @pl.loop(0, depth // K_LATER)
            def _(k):
                rows = pl.ds(pl.multiple_of(k * K_LATER, K_LATER), K_LATER)
                acc[:, here] += jnp.dot(
                    gt[:, rows], pbuf[rows, cols], preferred_element_type=F32
                )

        exchange(1, i, first, size)
        if i > 0:
            scatter(1, i - 1, *spans[-1])
        if i == 2:
            forward_w()
        if i == 3:
            await_w()
            absorb(0, 0, 0, sketch)
            spread(0)
        spans.append((first, size))
        first += size
    last = len(spans) - 1
    scatter(1, last, *spans[last])
    for i in range(last + 1):
        absorb(1, i, *spans[i])
    spread(1)
    pass_all(0)
    forward_rows(0)
    pass_all(1)
    await_rows(0)
    forward_rows(1)
    for q, c, l in passed:

        @pl.when(q == p)
        def _(l=l):
            l.wait()

        @pl.when(q != p)
        def _(c=c):
            c.wait_send()

    for slot in range(tile // piece):
        source = ((p * tile) % hw) // piece + slot
        dst = col.at[pl.ds(slot * piece, piece), :]

        @pl.when(source % n_p != p)
        def _(slot=slot, dst=dst):
            remote(
                row_block(0, p), dst, c_send.at[0, 0], c_recv.at[slot], {"param": partner}
            ).wait_recv()

    def product(h):
        out_ref[pl.ds(h * hw, hw), :] = lax.dot_general(
            row[h], col[...], (((1,), (1,)), ((), ())), preferred_element_type=F32
        ) * (1.0 / sketch)

    product(0)
    await_rows(1)
    product(1)
    for c in started:
        c.wait_send()


def solution(mesh):
    n_p, n_e = mesh.shape["param"], mesh.shape["ex"]

    def body(grads, projection, whitener):
        depth, width = grads.shape
        sketch = projection.shape[1]
        hw = width // HALVES
        piece = hw // n_p
        tile = width * n_e // n_p
        nk = depth // K_BLOCK
        dma = pltpu.SemaphoreType.DMA
        norm = 1.0 / math.sqrt(depth * n_p)
        chips = n_p // 2
        steps = len(B_CHUNKS)
        return pl.pallas_call(
            functools.partial(kernel, n_p, n_e, norm),
            out_shape=jax.ShapeDtypeStruct((width, tile), F32),
            in_specs=[pl.BlockSpec(memory_space=pl.ANY)] * 3,
            out_specs=pl.BlockSpec(memory_space=pltpu.VMEM),
            scratch_shapes=[
                pltpu.VMEM((HALVES, depth, hw), F32),
                pltpu.VMEM((depth, sketch), BF16),
                pltpu.VMEM((hw, depth), BF16),
                pltpu.VMEM((hw, sketch), F32),
                pltpu.VMEM((HALVES, hw // 2, sketch), F32),
                pltpu.VMEM((HALVES, hw // 2, sketch), F32),
                pltpu.VMEM((HALVES, hw // 2, sketch), F32),
                pltpu.VMEM((HALVES, hw // 2, sketch), BF16),
                pltpu.VMEM((HALVES, chips, piece, sketch), BF16),
                pltpu.VMEM(whitener.shape, F32),
                pltpu.VMEM((sketch, sketch), BF16),
                pltpu.VMEM((HALVES, piece, sketch), F32),
                pltpu.VMEM((HALVES, hw, sketch), BF16),
                pltpu.VMEM((HALVES, n_e, piece, sketch), BF16),
                pltpu.VMEM((tile, sketch), BF16),
                dma((HALVES, nk)), dma((nk,)), dma,
                dma((HALVES, steps)), dma((HALVES, steps)),
                dma((HALVES, steps, chips)), dma((HALVES, steps, chips)),
                dma((chips,)), dma((n_p,)), dma((chips,)), dma((n_p,)),
                dma((HALVES, chips)), dma((HALVES, n_p)),
                dma((HALVES, chips)), dma((HALVES, n_p)),
                dma((HALVES, n_e)), dma((HALVES, n_e)),
                dma((HALVES, n_e)), dma((tile // piece,)), dma((HALVES, n_e)),
            ],
            compiler_params=pltpu.CompilerParams(
                collective_id=0, has_side_effects=True, vmem_limit_bytes=67043328
            ),
        )(grads, projection, whitener)

    return jax.shard_map(
        body,
        mesh=mesh,
        in_specs=(P("param", "ex"), P("param", None), P("param", None)),
        out_specs=P("ex", "param"),
        check_vma=False,
    )
```
